32 devices in a mesh: groups: 2 (over x), seq: 8 (over z, y), tensor: 2 (over core).
Axes of the slice: x: 2, y: 2, z: 4, core: 2. Of those that a mesh axis runs over, the one named last changes fastest.
Arguments:
- patches: bfloat16 [6144, 1152], P(('groups', 'seq')), parts along dimension 0, may hold values from -6 to 6
- vis_up: bfloat16 [1152, 4304], P(None, 'tensor'), may hold values from -0.1875 to 0.1875
- vis_down: bfloat16 [4304, 1152], P('tensor'), may hold values from -0.09375 to 0.09375
- merge_weight: bfloat16 [4608, 5120], P('seq', 'tensor'), may hold values from -0.09375 to 0.09375
- text_states: bfloat16 [3072, 5120], P(('groups', 'seq'), 'tensor'), parts along dimension 0, may hold values from -6 to 6
- w_query: bfloat16 [5120, 4096], P('seq', 'tensor'), may hold values from -2.5 to 2.5, as said below
- w_key: bfloat16 [5120, 512], P('seq', 'tensor'), may hold values from -2.5 to 2.5, as said below
- w_value: bfloat16 [5120, 512], P('seq', 'tensor'), may hold values from -0.078125 to 0.078125
- dest_rows: int32 [1536], P(('groups', 'seq')), parts along dimension 0, may hold values from 0 to 1535, as said below
- doc_ids: int32 [3072], P(('groups', 'seq')), parts along dimension 0, may hold values from 0 to 3, never falling along the last dimension, each value on 1 to 768 neighbouring positions
Outputs:
- attended: bfloat16 [3072, 4096], P(('groups', 'seq'), 'tensor'), parts along dimension 0
The draws below stay inside these ranges and needn't reach their ends.
There are 2 independent parts, one for each index of `groups`. The reference program is written for one: setup_inputs(seed, part) draws one part's arguments, and reference() takes and returns one part's arrays. A program takes and returns all parts, laid end to end along the dimension named above; an argument that names none is the same for every part. Nothing has to cross between parts.
Inputs may be any that keep to these rules, and one draw needn't show every extreme that they name: `dest_rows`: all entries are distinct; each text shard of 192 positions receives exactly 96 of them; at most 24 of the rows of one seq shard go to one text shard, and some pair reaches 24 in every draw. `w_query`: A query projection of order 5120 ** -0.5 per entry. `w_key`: A key projection of order 5120 ** -0.5 per entry.
All inputs are finite; a program needn't handle non-finite values.
Results may differ from the reference program's by a relative error of at most 0.03.
Values may be sent and summed in bfloat16 or wider, within the bound.
No kernel may reach another device: no remote copies, remote signals or barrier semaphores. Data moves between devices by JAX's collectives and lax.ppermute only.
A program may use at most 128 MiB of HBM per device.

```python
import math
import jax
import jax.numpy as jnp
import numpy as np
from jax import lax

VD = 1152
VF = 4304
D = 5120
HEADS = 32
KVH = 4
HD = 128
MD = 4608
M_DEV = 96
TXT_DEV = 192
PATCHES = 3072
MERGED = 768
TEXT = 1536
N_SEQ = 8


def draw_w_query(key, part):
    base = jax.random.truncated_normal(jax.random.fold_in(key, 21), -4.0, 4.0, (D, HEADS * HD), jnp.float32) * D ** (-0.5)
    return base.astype(jnp.bfloat16)


def draw_w_key(key, part):
    base = jax.random.truncated_normal(jax.random.fold_in(key, 23), -4.0, 4.0, (D, KVH * HD), jnp.float32) * D ** (-0.5)
    return base.astype(jnp.bfloat16)


def draw_dest_rows(key, part):
    shards = N_SEQ
    base = M_DEV // shards
    subkeys = jax.random.split(jax.random.fold_in(key, 31), 5)
    picked = jax.random.permutation(subkeys[0], shards)
    extra = jax.random.randint(subkeys[1], (), 0, base)
    shard_index = jnp.arange(shards, dtype=jnp.int32)

    def marked(which):
        return (shard_index == picked[which]).astype(jnp.int32)
    loads = base + base * (marked(0) - marked(1)) + extra * (marked(2) - marked(3))
    shuffle = jax.random.permutation(subkeys[2], shards)
    counts = loads[(shuffle[None, :] - shard_index[:, None]) % shards]
    running = jnp.cumsum(counts, axis=0)
    slot_index = jnp.arange(M_DEV, dtype=jnp.int32)
    source = jnp.sum((running[:, :, None] <= slot_index[None, None, :]).astype(jnp.int32), axis=0)
    places = jax.vmap(lambda sub: jax.random.permutation(sub, TXT_DEV)[:M_DEV])(jax.random.split(subkeys[3], shards))
    flat_source = source.reshape(-1)
    serial = jnp.arange(MERGED, dtype=jnp.int32)
    same_before = (flat_source[None, :] == flat_source[:, None]) & (serial[None, :] < serial[:, None])
    slot_rank = jnp.sum(same_before.astype(jnp.int32), axis=1)
    orders = jax.vmap(lambda sub: jax.random.permutation(sub, M_DEV))(jax.random.split(subkeys[4], shards))
    row_in_source = orders[flat_source, slot_rank]
    target = (shard_index[:, None] * TXT_DEV + places).reshape(-1).astype(jnp.int32)
    return jnp.zeros((MERGED,), jnp.int32).at[flat_source * M_DEV + row_in_source].set(target)


def shard_levels(key, shape, cuts, low, largest):
    def one(axis_at, parts):
        draws = jax.random.uniform(jax.random.fold_in(jax.random.fold_in(key, 6), axis_at), (parts,), jnp.float32, low / len(cuts), largest / len(cuts))
        return jnp.repeat(jnp.exp(draws), shape[axis_at] // parts).reshape((-1,) + (1,) * (len(shape) - axis_at - 1))

    factor_of = one(*cuts[0])
    for cut in cuts[1:]:
        factor_of = factor_of * one(*cut)
    return factor_of


def profile(number_of, total, bound, lean):
    portions = [(1 << 20) // math.isqrt(standing ** lean) + 1 for standing in range(2, number_of + 1)]
    rest, given = total - bound - (number_of - 1), [1] * (number_of - 1)
    while rest > 0:
        candidates = [i for i in range(number_of - 1) if given[i] < bound]
        whole, remaining = sum([portions[i] for i in candidates]), rest
        for i in candidates:
            addition = min(bound - given[i], max(1, remaining * portions[i] // whole), rest)
            given[i] = given[i] + addition
            rest = rest - addition
    return np.array([bound] + given)


def ragged(stream_key, number_of, total, bound, lean):
    if number_of == 2:
        one = jax.random.randint(stream_key, (), max(1, total - bound), min(bound, total - 1) + 1)
        return jnp.stack([one, total - one])
    lengths = jnp.asarray(profile(number_of, total, bound, lean), jnp.int32)
    pairs = (number_of - 1) // 2
    giver, receiver = lengths[1:1 + 2 * pairs:2], lengths[2:2 + 2 * pairs:2]
    margin = jnp.minimum(giver - 1, bound - receiver)
    moved = jax.random.randint(jax.random.fold_in(stream_key, 1), (pairs,), 0, 1 << 20) % (margin + 1)
    lengths = lengths.at[1:1 + 2 * pairs:2].set(giver - moved).at[2:2 + 2 * pairs:2].set(receiver + moved)
    return lengths[jax.random.permutation(jax.random.fold_in(stream_key, 2), number_of)]


def bell_draw(key, shape, deviation, reach, cuts=(), held_as=jnp.bfloat16):
    array = deviation * jax.random.normal(key, shape, jnp.float32)
    if cuts:
        array = array * shard_levels(key, shape, cuts, -0.22, 0.18)
    return jnp.clip(array, -reach, reach).astype(held_as)


def setup_inputs(seed: int = 0, part: int = 0) -> dict:
    streams_of = jax.random.split(jax.random.key(seed), 11)
    part_keys = jax.random.split(jax.random.fold_in(streams_of[10], part), 11)
    return {
        "patches": bell_draw(part_keys[0], (PATCHES, VD), 1.0, 6.0, ((0, 8),)),
        "vis_up": bell_draw(streams_of[1], (VD, VF), VD ** -0.5, 0.1875, ((1, 2),)),
        "vis_down": bell_draw(streams_of[2], (VF, VD), VF ** -0.5, 0.09375, ((0, 2),)),
        "merge_weight": bell_draw(streams_of[3], (MD, D), MD ** -0.5, 0.09375, ((0, 8), (1, 2))),
        "text_states": bell_draw(part_keys[4], (TEXT, D), 1.0, 6.0, ((0, 8), (1, 2))),
        "w_query": draw_w_query(jax.random.fold_in(streams_of[10], 71), part),
        "w_key": draw_w_key(jax.random.fold_in(streams_of[10], 71), part),
        "w_value": bell_draw(streams_of[7], (D, KVH * HD), D ** -0.5, 0.078125, ((0, 8), (1, 2))),
        "dest_rows": draw_dest_rows(jax.random.fold_in(jax.random.fold_in(streams_of[10], part), 71), part),
        "doc_ids": jnp.searchsorted(jnp.cumsum(ragged(part_keys[9], 4, TEXT, TEXT // 2, 0)), jnp.arange(TEXT), side="right").astype(jnp.int32),
    }


epsilon = 1e-06

def layer_norm(values):
    center = lax.optimization_barrier(jnp.mean(values, axis=-1, keepdims=True))
    spread = lax.optimization_barrier(jnp.mean((values - center) ** 2, axis=-1, keepdims=True))
    return (values - center) * lax.rsqrt(spread + epsilon)

def reference(patches, vis_up, vis_down, merge_weight, text_states, w_query, w_key, w_value, dest_rows, doc_ids):
    values = patches.astype(jnp.float32)
    normed = layer_norm(values).astype(jnp.bfloat16)
    activated = jax.nn.gelu(jnp.dot(normed, vis_up, preferred_element_type=jnp.float32), approximate=True).astype(jnp.bfloat16)
    vision_out = values + jnp.dot(activated, vis_down, preferred_element_type=jnp.float32)
    grouped = layer_norm(vision_out.reshape(MERGED, MD)).astype(jnp.bfloat16)
    block_width = MD // N_SEQ

    def block_sum(running, index):
        offset = (index * block_width).astype(jnp.int32)
        columns = lax.dynamic_slice_in_dim(grouped, offset, block_width, 1)
        weight_rows = lax.dynamic_slice_in_dim(merge_weight, offset, block_width, 0)
        partial_value = jnp.dot(columns, weight_rows, preferred_element_type=jnp.float32)
        rounded = lax.optimization_barrier(partial_value.astype(jnp.bfloat16))
        return (running + rounded.astype(jnp.float32), None)
    merged, _ = lax.scan(block_sum, jnp.zeros((MERGED, D), jnp.float32), jnp.arange(N_SEQ, dtype=jnp.int32))
    merged = merged.astype(jnp.bfloat16)
    routed = jnp.zeros((TEXT, D), jnp.bfloat16).at[dest_rows].set(merged)
    mixed = text_states.astype(jnp.float32) + routed.astype(jnp.float32)
    normed_text = (mixed * lax.rsqrt(lax.optimization_barrier(jnp.mean(mixed * mixed, axis=-1, keepdims=True)) + epsilon)).astype(jnp.bfloat16)
    queries = jnp.dot(normed_text, w_query, preferred_element_type=jnp.float32).astype(jnp.bfloat16)
    keys_all = jnp.dot(normed_text, w_key, preferred_element_type=jnp.float32).astype(jnp.bfloat16)
    values_all = jnp.dot(normed_text, w_value, preferred_element_type=jnp.float32).astype(jnp.bfloat16)
    query_heads = queries.reshape(TEXT, HEADS, HD)
    key_heads = keys_all.reshape(TEXT, KVH, HD)
    value_heads = values_all.reshape(TEXT, KVH, HD)
    group_size = HEADS // KVH
    positions = jnp.arange(TEXT, dtype=jnp.int32)
    visible = (positions[None, :] <= positions[:, None]) & (doc_ids[None, :] == doc_ids[:, None])
    score_scale = HD ** (-0.5)

    def per_head(head):
        query_one = lax.dynamic_index_in_dim(query_heads, head, 1, keepdims=False)
        key_one = lax.dynamic_index_in_dim(key_heads, head // group_size, 1, keepdims=False)
        value_one = lax.dynamic_index_in_dim(value_heads, head // group_size, 1, keepdims=False)
        scores = jnp.dot(query_one, key_one.T, preferred_element_type=jnp.float32) * score_scale
        highest = lax.optimization_barrier(jnp.max(jnp.where(visible, scores, -1e+30), axis=-1, keepdims=True))
        raw = jnp.where(visible, jnp.exp(scores - highest), 0.0)
        mass = lax.optimization_barrier(jnp.sum(raw, axis=-1, keepdims=True))
        summed = jnp.dot(raw.astype(jnp.bfloat16), value_one, preferred_element_type=jnp.float32)
        return (summed / mass).astype(jnp.bfloat16)
    heads_out = lax.map(per_head, jnp.arange(HEADS, dtype=jnp.int32))
    return jnp.transpose(heads_out, (1, 0, 2)).reshape(TEXT, HEADS * HD)
```

```python
import jax
import jax.numpy as jnp
from jax import lax
from jax.experimental import pallas as pl
from jax.experimental.pallas import tpu as pltpu
from jax.sharding import PartitionSpec as P

HD = 128
epsilon = 1e-06
bf16 = jnp.bfloat16
f32 = jnp.float32
SWAP = [(0, 1), (1, 0)]


def layer_norm(values, axes):
    center = jnp.mean(values, axis=axes, keepdims=True)
    spread = jnp.mean((values - center) ** 2, axis=axes, keepdims=True)
    return (values - center) * lax.rsqrt(spread + epsilon)


def pick(blocks, index, axis=0):
    return lax.dynamic_index_in_dim(blocks, index, axis, keepdims=False)


def plus(first, second):
    return (first.astype(f32) + second.astype(f32)).astype(bf16)


def attend_kernel(q_ref, rinv_ref, k_ref, v_ref, qdoc_ref, kdoc_ref, o_ref, bias_ref):
    rows, span = bias_ref.shape

    @pl.when(pl.program_id(0) == 0)
    def _():
        column = lax.broadcasted_iota(jnp.int32, (rows, span), 1)
        row = lax.broadcasted_iota(jnp.int32, (rows, span), 0)
        visible = (qdoc_ref[...] == kdoc_ref[...]) & (column <= row + (span - rows))
        bias_ref[...] = jnp.where(visible, 0.0, -1e30)

    query = (q_ref[...].astype(f32) * rinv_ref[...]).astype(bf16)
    scores = lax.dot_general(
        query, k_ref[...], (((1,), (1,)), ((), ())), preferred_element_type=f32
    ) * (HD**-0.5) + bias_ref[...]
    top = jnp.max(scores, axis=-1, keepdims=True)
    raw = jnp.exp(scores - top)
    mass = jnp.sum(raw, axis=-1, keepdims=True)
    summed = jnp.dot(raw.astype(bf16), v_ref[...], preferred_element_type=f32)
    o_ref[...] = (summed / mass).astype(bf16)


def attend(query, rinv, window, qdoc, kdoc):
    rows, width = query.shape
    span, both = window.shape
    heads, kv_heads = width // HD, both // (2 * HD)
    ratio = heads // kv_heads
    return pl.pallas_call(
        attend_kernel,
        grid=(heads,),
        in_specs=[
            pl.BlockSpec((rows, HD), lambda h: (0, h)),
            pl.BlockSpec((rows, 1), lambda h: (0, 0)),
            pl.BlockSpec((span, HD), lambda h: (0, h // ratio)),
            pl.BlockSpec((span, HD), lambda h: (0, kv_heads + h // ratio)),
            pl.BlockSpec((rows, 1), lambda h: (0, 0)),
            pl.BlockSpec((1, span), lambda h: (0, 0)),
        ],
        out_specs=pl.BlockSpec((rows, HD), lambda h: (0, h)),
        out_shape=jax.ShapeDtypeStruct((rows, width), bf16),
        scratch_shapes=[pltpu.VMEM((rows, span), f32)],
        compiler_params=pltpu.CompilerParams(vmem_limit_bytes=32 * 2**20),
    )(query, rinv, window, window, qdoc, kdoc)


def body(
    patches,
    vis_up,
    vis_down,
    merge_weight,
    text_states,
    w_query,
    w_key,
    w_value,
    dest_rows,
    doc_ids,
):
    n = lax.axis_size("seq")
    group_count = lax.axis_size("groups")
    assert lax.axis_size("tensor") == 2 and n % 2 == 0
    levels, half = n // 2, n // 2
    s, t, g = lax.axis_index("seq"), lax.axis_index("tensor"), lax.axis_index("groups")
    z, y = s // 2, s % 2
    pairs = [(i, i ^ 1) for i in range(n)]
    lines = [[2 * level + side for level in range(levels)] for side in range(2)]

    def across(value):
        return lax.ppermute(value, "tensor", SWAP)

    def sideways(value):
        return lax.ppermute(value, "seq", pairs)

    def line_reduce(value):
        return lax.psum_scatter(
            value, "seq", scatter_dimension=0, tiled=True, axis_index_groups=lines
        )

    patch_rows, vision_width = patches.shape
    merged_rows = patch_rows // 4
    text_rows, half_width = text_states.shape
    shard = w_query.shape[0]
    query_cols, kv_cols = w_query.shape[1], w_key.shape[1]
    block = merge_weight.shape[0]
    assert text_rows <= 256 and merged_rows % 2 == 0

    if group_count % 2 == 0:
        cut = shard // 2
        start = (g % 2) * cut
        piece = jnp.concatenate(
            [lax.dynamic_slice_in_dim(w, start, cut, 0) for w in (w_query, w_key, w_value)], axis=1
        )
        near = sideways(piece)
        far = lax.ppermute(near, "groups", [(i, i ^ 1) for i in range(group_count)])
        even = g % 2 == 0
        other_weights = jnp.concatenate(
            [jnp.where(even, near, far), jnp.where(even, far, near)], axis=0
        )
    else:
        other_weights = sideways(jnp.concatenate([w_query, w_key, w_value], axis=1))

    values = patches.astype(f32)
    normed = layer_norm(values, (1,)).astype(bf16)
    activated = jax.nn.gelu(
        jnp.dot(normed, vis_up, preferred_element_type=f32), approximate=True
    ).astype(bf16)
    partial = jnp.dot(activated, vis_down, preferred_element_type=f32).astype(bf16)
    half_rows = patch_rows // 2
    mine = lax.dynamic_slice_in_dim(partial, t * half_rows, half_rows, 0)
    theirs = lax.dynamic_slice_in_dim(partial, (1 - t) * half_rows, half_rows, 0)
    own_patches = lax.dynamic_slice_in_dim(patches, t * half_rows, half_rows, 0)
    vision_out = own_patches.astype(f32) + (mine.astype(f32) + across(theirs).astype(f32))
    half_merged = merged_rows // 2
    grouped = layer_norm(vision_out.reshape(half_merged, 4, vision_width), (1, 2)).astype(bf16)

    blocks = grouped.reshape(half_merged, n, block).transpose(1, 0, 2)
    spare = 128 - block % 128
    my_dest = lax.dynamic_slice_in_dim(dest_rows, t * half_merged, half_merged, 0)
    docs_per_row = text_rows // merged_rows
    my_docs = lax.dynamic_slice_in_dim(doc_ids, t * (text_rows // 2), text_rows // 2, 0)
    notes = jnp.concatenate(
        [
            (my_dest // text_rows)[:, None],
            (my_dest % text_rows)[:, None],
            my_docs.reshape(half_merged, docs_per_row),
        ],
        axis=1,
    ).astype(bf16)
    notes = jnp.pad(notes, ((0, 0), (0, spare - notes.shape[1])))
    payload = jnp.concatenate(
        [blocks, jnp.broadcast_to(notes[None], (n,) + notes.shape)], axis=2
    )
    width = block + spare
    twice = jnp.concatenate([payload, payload], axis=0)
    by_shift = lax.dynamic_slice_in_dim(twice, s + 1, n, 0).reshape(2, half, half_merged, width)
    kept = pick(by_shift, t)
    full = jnp.concatenate([kept, across(pick(by_shift, 1 - t))], axis=1)
    arrived = []
    for j in range(half):
        route = [
            (2 * i + core, 2 * ((i + 1 + j + half * core) % n) + core)
            for i in range(n)
            for core in range(2)
        ]
        arrived.append(lax.ppermute(full[j], ("seq", "tensor"), route))
    arrived = jnp.stack(arrived)
    gathered = jnp.stack([arrived, across(arrived)])
    near_notes = pick(gathered[..., block:], t)
    columns = gathered.reshape(n * merged_rows, width)
    destinations = columns[:, block].astype(jnp.int32) * text_rows + columns[
        :, block + 1
    ].astype(jnp.int32)
    slots = n * merged_rows
    rank = jnp.sum(
        (destinations[:, None] < destinations[None, :]).astype(jnp.int32), axis=0
    )
    sorter = (jnp.arange(slots, dtype=jnp.int32)[:, None] == rank[None, :]).astype(bf16)
    ordered = jnp.dot(sorter, columns[:, :block], preferred_element_type=f32).astype(bf16)

    def pair_reduce_first(weight):
        product = jnp.dot(ordered, weight, preferred_element_type=f32).astype(bf16)
        product = product.reshape(levels, 2, merged_rows, weight.shape[1])
        total = plus(pick(product, y, 1), sideways(pick(product, 1 - y, 1)))
        return line_reduce(total.reshape(levels * merged_rows, weight.shape[1]))

    def line_reduce_first(weight):
        product = jnp.dot(ordered, weight, preferred_element_type=f32).astype(bf16)
        total = line_reduce(product).reshape(2, merged_rows, weight.shape[1])
        return plus(pick(total, y), sideways(pick(total, 1 - y)))

    tiles = half_width // 128
    cuts = [0, tiles // 4 * 128, tiles * 13 // 20 * 128, half_width]
    merged = jnp.concatenate(
        [
            line_reduce_first(merge_weight[:, cuts[0] : cuts[1]]),
            pair_reduce_first(merge_weight[:, cuts[1] : cuts[2]]),
            pair_reduce_first(merge_weight[:, cuts[2] : cuts[3]]),
        ],
        axis=1,
    )
    positions = s * text_rows + jnp.arange(text_rows, dtype=jnp.int32)
    present = jnp.any(positions[:, None] == destinations[None, :], axis=1)
    before = (
        jnp.sum((destinations[None, :] < positions[:, None]).astype(jnp.int32), axis=1)
        - s * merged_rows
    )
    placer = (
        present[:, None]
        & (before[:, None] == jnp.arange(merged_rows, dtype=jnp.int32)[None, :])
    ).astype(bf16)
    routed = jnp.dot(placer, merged, preferred_element_type=f32)
    mixed = text_states.astype(f32) + routed
    squares = jnp.sum(mixed * mixed, axis=1, keepdims=True)
    squares = squares + across(squares)
    rinv = lax.rsqrt(squares / (2 * half_width) + epsilon)
    mixed = mixed.astype(bf16)

    text_half = text_rows // 2
    stay = lax.dynamic_slice_in_dim(mixed, t * text_half, text_half, 0)
    leave = lax.dynamic_slice_in_dim(mixed, (1 - t) * text_half, text_half, 0)
    both = jnp.stack([stay, across(leave)])
    per_core = n // 2
    feature_blocks = both.reshape(2, text_half, per_core, shard)
    feature_blocks = feature_blocks.transpose(0, 2, 1, 3).reshape(n, text_half, shard)

    def for_level(level):
        def one(owner):
            return pick(feature_blocks, (owner + t * per_core) % n)

        return jnp.concatenate([one(2 * level + y), one(2 * level + 1 - y)], axis=1)

    received = [for_level(z)]
    for k in range(1, levels):
        route = [
            (2 * level + side, 2 * ((level + k) % levels) + side)
            for level in range(levels)
            for side in range(2)
        ]
        received.append(lax.ppermute(for_level((z + k) % levels), "seq", route))
    received = jnp.stack(received)
    shared = jnp.stack([received, across(received)])
    low, high = pick(shared, t), pick(shared, 1 - t)
    rows = jnp.concatenate([low, high], axis=1)
    backward = rows[::-1]
    rows = lax.dynamic_slice_in_dim(
        jnp.concatenate([backward, backward], axis=0), levels - 1 - z, levels, 0
    ).reshape(levels * text_rows, 2 * shard)

    def project(mine, other):
        return (
            jnp.dot(rows[:, :shard], mine, preferred_element_type=f32)
            + jnp.dot(rows[:, shard:], other, preferred_element_type=f32)
        ).astype(bf16)

    kv_sum = line_reduce(
        project(jnp.concatenate([w_key, w_value], axis=1), other_weights[:, query_cols:])
    )
    query_sum = line_reduce(project(w_query, other_weights[:, :query_cols]))
    kv = (kv_sum.astype(f32) * rinv).astype(bf16)

    window, window_docs = [kv], [doc_ids]
    near_docs = near_notes[:, :, 2 : 2 + docs_per_row].reshape(half, text_rows).astype(jnp.int32)
    for k in range(1, half + 1):
        window.append(lax.ppermute(kv, "seq", [(i, i + k) for i in range(n - k)]))
        window_docs.append(jnp.where(s >= k, near_docs[k - 1], -1))
    window = jnp.concatenate(window[::-1], axis=0)
    window_docs = jnp.concatenate(window_docs[::-1])
    return attend(query_sum, rinv, window, doc_ids[:, None], window_docs[None, :])


def solution(mesh):
    in_specs = (
        P(("groups", "seq"), None),
        P(None, "tensor"),
        P("tensor", None),
        P("seq", "tensor"),
        P(("groups", "seq"), "tensor"),
        P("seq", "tensor"),
        P("seq", "tensor"),
        P("seq", "tensor"),
        P(("groups", "seq")),
        P(("groups", "seq")),
    )
    out_specs = P(("groups", "seq"), "tensor")
    return jax.shard_map(body, mesh=mesh, in_specs=in_specs, out_specs=out_specs, check_vma=False)
```
